128 devices in a mesh: tm: 16 (over y, x), ops: 8 (over z, core).
Axes of the slice: x: 4, y: 4, z: 4, core: 2. Of those that a mesh axis runs over, the one named last changes fastest.
Arguments:
- node_blocks: bfloat16 [512, 384, 768], P(('tm', 'ops')), may hold values from -6 to 6
- first_pulls: int32 [128, 16], replicated, may hold values from 0 to 511, as said below
- first_left: int32 [128, 24], replicated, may hold values from 0 to 15
- first_right: int32 [128, 24], replicated, may hold values from 0 to 15
- first_live: int32 [128], replicated, may hold values from 1 to 24, as said below
- second_pulls: int32 [128, 16], replicated, may hold values from 0 to 3071, as said below
- second_left: int32 [128, 16], replicated, may hold values from 0 to 15
- second_right: int32 [128, 16], replicated, may hold values from 0 to 15
- second_live: int32 [128], replicated, may hold values from 1 to 16, as said below
- diagram_ids: int32 [128, 16], replicated, may hold values from 0 to 127, as said below
- diagram_signs: int32 [128, 16], replicated, may hold values from -1 to 1, as said below
Outputs:
- diagrams: float32 [128, 384, 768], P(('tm', 'ops'))
The draws below stay inside these ranges and needn't reach their ends.
Inputs may be any that keep to these rules, and one draw needn't show every extreme that they name: `first_pulls`: every node in row w belongs to a device with the same ops index as w. At most 1 entries of a row belong to any one device, and every row has a device with exactly 1. `first_live`: some worker has 24 pairs. `second_pulls`: each entry is an id h * 24 + p with p < first_live[h], where h is a device with the same tm index as w. At most 2 entries of a row belong to any one device h, and every row has a device with exactly 2. `second_live`: some worker has 16 pairs. `diagram_ids`: every diagram of row w is owned by a device with the same tm index as w. `diagram_signs`: each entry is +1 or -1.
All inputs are finite; a program needn't handle non-finite values.
Results may differ from the reference program's by a relative error of at most 0.004.
Values may be sent and summed in bfloat16 or wider, within the bound.
No kernel may reach another device: no remote copies, remote signals or barrier semaphores. Data moves between devices by JAX's collectives and lax.ppermute only.
A program may use at most 128 MiB of HBM per device.

```python
import math
import jax
import jax.numpy as jnp
from jax import lax

R = 384
NODE_DEV = 4
INP1 = 16
CAP1 = 24
INP2 = 16
CAP2 = 16
DIAG_DEV = 1
NODES = 512
DIAGS = 128
N_TM = 16
N_OPS = 8


def skewed_counts(key, top_count):
    worker_count = N_TM * N_OPS
    lower = jax.random.randint(jax.random.fold_in(key, 1), (worker_count,), 0, top_count)
    higher = jax.random.randint(jax.random.fold_in(key, 2), (worker_count,), 0, top_count)
    counts = 1 + jnp.minimum(lower, higher)
    busiest = jax.random.randint(jax.random.fold_in(key, 3), (), 0, worker_count)
    return jnp.where(jnp.arange(worker_count) == busiest, top_count, counts).astype(jnp.int32)


def first_counts(key):
    return skewed_counts(jax.random.fold_in(key, 101), CAP1)


def row_orders(key, length, reads):
    worker_count = N_TM * N_OPS
    row_keys = jax.random.split(key, worker_count)

    def one_row(row_key):
        return jax.random.permutation(row_key, length)
    orders = jax.vmap(one_row)(row_keys)
    return orders[:, jnp.arange(reads) % length]


def row_starts():
    worker_count = N_TM * N_OPS
    return (jnp.arange(worker_count) // N_OPS * N_OPS)[:, None]


def draw_first_pulls(key, part):
    worker_count = N_TM * N_OPS
    source_times = row_orders(jax.random.fold_in(key, 201), N_TM, INP1)
    node_slot = jax.random.randint(jax.random.fold_in(key, 202), (worker_count, INP1), 0, NODE_DEV)
    groups = (jnp.arange(worker_count) % N_OPS)[:, None]
    return ((source_times * N_OPS + groups) * NODE_DEV + node_slot).astype(jnp.int32)


def draw_first_left(key, part):
    return jax.random.randint(jax.random.fold_in(key, 203), (N_TM * N_OPS, CAP1), 0, INP1).astype(jnp.int32)


def draw_first_right(key, part):
    return jax.random.randint(jax.random.fold_in(key, 204), (N_TM * N_OPS, CAP1), 0, INP1).astype(jnp.int32)


def draw_first_live(key, part):
    return first_counts(key)


def draw_second_pulls(key, part):
    worker_count = N_TM * N_OPS
    counts = first_counts(key)
    source_groups = row_orders(jax.random.fold_in(key, 301), N_OPS, INP2)
    holders = row_starts() + source_groups
    raw_draws = jax.random.randint(jax.random.fold_in(key, 302), (worker_count, INP2), 0, 1 << 20)
    slot_draws = raw_draws % jnp.take(counts, holders)
    return (holders * CAP1 + slot_draws).astype(jnp.int32)


def draw_second_left(key, part):
    return jax.random.randint(jax.random.fold_in(key, 303), (N_TM * N_OPS, CAP2), 0, INP2).astype(jnp.int32)


def draw_second_right(key, part):
    return jax.random.randint(jax.random.fold_in(key, 304), (N_TM * N_OPS, CAP2), 0, INP2).astype(jnp.int32)


def draw_second_live(key, part):
    return skewed_counts(jax.random.fold_in(key, 401), CAP2)


def draw_diagram_ids(key, part):
    worker_count = N_TM * N_OPS
    groups = jax.random.randint(jax.random.fold_in(key, 501), (worker_count, CAP2), 0, N_OPS)
    within = jax.random.randint(jax.random.fold_in(key, 502), (worker_count, CAP2), 0, DIAG_DEV)
    return ((row_starts() + groups) * DIAG_DEV + within).astype(jnp.int32)


def draw_diagram_signs(key, part):
    coins = jax.random.randint(jax.random.fold_in(key, 601), (N_TM * N_OPS, CAP2), 0, 2)
    return (coins * 2 - 1).astype(jnp.int32)


def level_of(rng, extent, pieces, low, top_value):
    loudness, own = 1.0, jax.random.fold_in(rng, 6)
    for position, blocks in pieces:
        steps = jnp.exp(jax.random.uniform(jax.random.fold_in(own, position), (blocks,), jnp.float32, low / len(pieces), top_value / len(pieces)))
        loudness = loudness * jnp.repeat(steps, extent[position] // blocks).reshape([-1 if axis == position else 1 for axis in range(len(extent))])
    return loudness


def gaussian(key, extent, deviation, limit, shards=(), kind=jnp.bfloat16):
    drawn = jax.random.normal(key, extent, jnp.float32) * deviation
    if len(shards) > 0:
        drawn = level_of(key, extent, shards, -0.22, 0.18) * drawn
    return jnp.clip(drawn, min=-limit, max=limit).astype(kind)


def setup_inputs(seed: int = 0) -> dict:
    streams_of = jax.random.split(jax.random.key(seed), 12)
    return {
        "node_blocks": gaussian(streams_of[0], (NODES, R, 2 * R), 1.0, 6.0, ((0, 128),)),
        "first_pulls": draw_first_pulls(jax.random.fold_in(streams_of[11], 71), 0),
        "first_left": draw_first_left(jax.random.fold_in(streams_of[11], 71), 0),
        "first_right": draw_first_right(jax.random.fold_in(streams_of[11], 71), 0),
        "first_live": draw_first_live(jax.random.fold_in(streams_of[11], 71), 0),
        "second_pulls": draw_second_pulls(jax.random.fold_in(streams_of[11], 71), 0),
        "second_left": draw_second_left(jax.random.fold_in(streams_of[11], 71), 0),
        "second_right": draw_second_right(jax.random.fold_in(streams_of[11], 71), 0),
        "second_live": draw_second_live(jax.random.fold_in(streams_of[11], 71), 0),
        "diagram_ids": draw_diagram_ids(jax.random.fold_in(streams_of[11], 71), 0),
        "diagram_signs": draw_diagram_signs(jax.random.fold_in(streams_of[11], 71), 0),
    }


def complex_product(first_block, second_block):
    first_block = first_block.astype(jnp.float32)
    second_block = second_block.astype(jnp.float32)
    rank_size = first_block.shape[0]
    second_real = second_block[:, :rank_size]
    second_imag = second_block[:, rank_size:]
    upper_half = jnp.concatenate([second_real, second_imag], axis=1)
    lower_half = jnp.concatenate([-second_imag, second_real], axis=1)
    stacked = jnp.concatenate([upper_half, lower_half], axis=0)
    return jnp.dot(first_block, stacked, precision=lax.Precision.HIGHEST, preferred_element_type=jnp.float32)

def reference(node_blocks, first_pulls, first_left, first_right, first_live, second_pulls, second_left, second_right, second_live, diagram_ids, diagram_signs):
    rank_size = node_blocks.shape[1]
    norm_factor = 1.0 / math.sqrt(2.0 * rank_size)
    block_shape = (rank_size, 2 * rank_size)

    def first_worker(worker):
        pull_list = first_pulls[worker]
        live_count = first_live[worker]

        def first_pair(pair_index):
            first_block = node_blocks[pull_list[first_left[worker, pair_index]]]
            second_block = node_blocks[pull_list[first_right[worker, pair_index]]]
            live_mask = (pair_index < live_count).astype(jnp.float32)
            return (complex_product(first_block, second_block) * (norm_factor * live_mask)).astype(jnp.bfloat16)
        return lax.map(first_pair, jnp.arange(CAP1, dtype=jnp.int32))

    def time_row(time_row_index):
        row_workers = (time_row_index * N_OPS + jnp.arange(N_OPS)).astype(jnp.int32)
        stored = lax.map(first_worker, row_workers).reshape((N_OPS * CAP1,) + block_shape)
        row_base = time_row_index * N_OPS * CAP1
        pair_workers = jnp.repeat(row_workers, CAP2)
        pair_slots = jnp.tile(jnp.arange(CAP2, dtype=jnp.int32), N_OPS)

        def second_pair(diagram_total, pair_info):
            worker, slot_index = pair_info
            pull_list = second_pulls[worker] - row_base
            first_block = stored[pull_list[second_left[worker, slot_index]]]
            second_block = stored[pull_list[second_right[worker, slot_index]]]
            live_mask = (slot_index < second_live[worker]).astype(jnp.float32)
            weight = diagram_signs[worker, slot_index].astype(jnp.float32) * live_mask
            signed_term = complex_product(first_block, second_block) * norm_factor * weight
            target = diagram_ids[worker, slot_index] - time_row_index * N_OPS * DIAG_DEV
            return (diagram_total.at[target].add(signed_term), None)
        result = lax.scan(second_pair, jnp.zeros((N_OPS * DIAG_DEV,) + block_shape, jnp.float32), (pair_workers, pair_slots))
        return result[0]
    per_row = lax.map(time_row, jnp.arange(N_TM, dtype=jnp.int32))
    return per_row.reshape((DIAGS,) + block_shape)
```

```python
import math

import jax
import jax.numpy as jnp
from jax import lax
from jax.experimental import pallas as pl
from jax.experimental.pallas import tpu as pltpu
from jax.sharding import PartitionSpec as P

ANY = pl.BlockSpec(memory_space=pl.ANY)


def column(table, index):
    turned = table.T
    return lax.dynamic_slice_in_dim(turned, index, 1, axis=1)[:, 0]


def look_up(values, keys):
    hits = keys[:, None] == jnp.arange(values.shape[0])[None, :]
    return jnp.sum(jnp.where(hits, values[None, :], 0), axis=1)


def stack_right(block, stacked, rank):
    stacked[:rank, :] = block[...]
    stacked[rank:, :rank] = -block[:, rank:]
    stacked[rank:, rank:] = block[:, :rank]


def pick_blocks(slots, nodes):
    count = slots.shape[0]

    def kernel(slot_ref, nodes_ref, out_ref, sems):
        copies = [
            pltpu.make_async_copy(nodes_ref.at[slot_ref[i]], out_ref.at[i], sems.at[i])
            for i in range(count)
        ]
        for copy in copies:
            copy.start()
        for copy in copies:
            copy.wait()

    return pl.pallas_call(
        kernel,
        out_shape=jax.ShapeDtypeStruct((count,) + nodes.shape[1:], nodes.dtype),
        in_specs=[
            pl.BlockSpec(memory_space=pltpu.SMEM),
            pl.BlockSpec(memory_space=pltpu.VMEM),
        ],
        out_specs=ANY,
        scratch_shapes=[pltpu.SemaphoreType.DMA((count,))],
        name="pick_blocks",
    )(slots, nodes)


def pair_products(left, right, blocks, norm):
    count = left.shape[0]
    rank, width = blocks.shape[1:]

    def kernel(left_ref, right_ref, a_ref, b_ref, out_ref, stacked):
        stack_right(b_ref, stacked, rank)
        product = jnp.dot(a_ref[...], stacked[...], preferred_element_type=jnp.float32)
        out_ref[...] = (product * norm).astype(out_ref.dtype)

    block = (None, rank, width)
    return pl.pallas_call(
        kernel,
        out_shape=jax.ShapeDtypeStruct((count, rank, width), jnp.bfloat16),
        grid_spec=pltpu.PrefetchScalarGridSpec(
            num_scalar_prefetch=2,
            grid=(count,),
            in_specs=[
                pl.BlockSpec(block, lambda i, l, r: (l[i], 0, 0)),
                pl.BlockSpec(block, lambda i, l, r: (r[i], 0, 0)),
            ],
            out_specs=pl.BlockSpec(block, lambda i, l, r: (i, 0, 0)),
            scratch_shapes=[pltpu.VMEM((width, width), jnp.bfloat16)],
        ),
        name="pair_products",
    )(left, right, blocks, blocks)


def signed_sums(left, right, target, sign, live, blocks, norm, targets):
    count = left.shape[0]
    rank, width = blocks.shape[1:]

    def kernel(left_ref, right_ref, target_ref, sign_ref, live_ref, a_ref, b_ref, out_ref, stacked):
        step = pl.program_id(0)

        @pl.when(step == 0)
        def _():
            out_ref[...] = jnp.zeros_like(out_ref)

        @pl.when(step < live_ref[0])
        def _():
            stack_right(b_ref, stacked, rank)
            product = jnp.dot(a_ref[...], stacked[...], preferred_element_type=jnp.float32)
            weight = sign_ref[step].astype(jnp.float32) * norm
            out_ref[target_ref[step]] += product * weight

    def pick(index_of):
        def index(i, l, r, t, s, n):
            return (index_of(l, r)[jnp.minimum(i, n[0] - 1)], 0, 0)

        return pl.BlockSpec((None, rank, width), index)

    return pl.pallas_call(
        kernel,
        out_shape=jax.ShapeDtypeStruct((targets, rank, width), jnp.float32),
        grid_spec=pltpu.PrefetchScalarGridSpec(
            num_scalar_prefetch=5,
            grid=(count,),
            in_specs=[pick(lambda l, r: l), pick(lambda l, r: r)],
            out_specs=pl.BlockSpec(
                (targets, rank, width),
                lambda i, l, r, t, s, n: (0, 0, 0),
                pipeline_mode=pl.Buffered(1),
            ),
            scratch_shapes=[pltpu.VMEM((width, width), jnp.bfloat16)],
        ),
        compiler_params=pltpu.CompilerParams(vmem_limit_bytes=40 << 20),
        name="signed_sums",
    )(left, right, target, sign, live, blocks, blocks)


def body(
    node_blocks,
    first_pulls,
    first_left,
    first_right,
    first_live,
    second_pulls,
    second_left,
    second_right,
    second_live,
    diagram_ids,
    diagram_signs,
):
    times = lax.axis_size("tm")
    groups = lax.axis_size("ops")
    time = lax.axis_index("tm")
    group = lax.axis_index("ops")
    worker = time * groups + group
    held, rank = node_blocks.shape[:2]
    norm = 1.0 / math.sqrt(2.0 * rank)
    cap = first_left.shape[1]

    pulls = lax.dynamic_slice_in_dim(
        first_pulls.T.reshape(first_pulls.shape[1], times, groups), group, 1, axis=2
    )[:, :, 0]
    slots = jnp.sum(jnp.where(pulls // held == worker, pulls % held, 0), axis=0)
    outgoing = pick_blocks(slots, node_blocks)
    nodes = lax.all_to_all(outgoing, "tm", split_axis=0, concat_axis=0, tiled=True)

    source_time = column(first_pulls, worker) // held // groups
    pair_left = look_up(source_time, column(first_left, worker))
    pair_right = look_up(source_time, column(first_right, worker))
    row_pulls = lax.dynamic_slice_in_dim(second_pulls.T, time * groups, groups, axis=1)
    reads = second_pulls.shape[1]
    coded = jnp.arange(reads)[:, None] * 64 + row_pulls % cap
    mine = row_pulls // cap == worker
    first_pair = jnp.min(jnp.where(mine, coded, reads * 64), axis=0) % 64
    last_pair = jnp.max(jnp.where(mine, coded, 0), axis=0) % 64
    wanted = jnp.stack([first_pair, last_pair], axis=1).reshape(-1)
    products = pair_products(
        look_up(pair_left, wanted), look_up(pair_right, wanted), nodes, norm
    )
    factors = lax.all_to_all(products, "ops", split_axis=0, concat_axis=0, tiled=True)

    source_group = column(second_pulls, worker) // cap % groups
    earlier = jnp.arange(reads)[:, None] > jnp.arange(reads)[None, :]
    again = jnp.any(
        jnp.logical_and(source_group[:, None] == source_group[None, :], earlier), axis=1
    )
    place = source_group * 2 + again.astype(jnp.int32)
    target = column(diagram_ids, worker) - time * groups
    live = lax.dynamic_slice_in_dim(second_live, worker, 1)
    sums = signed_sums(
        look_up(place, column(second_left, worker)),
        look_up(place, column(second_right, worker)),
        target,
        column(diagram_signs, worker),
        live,
        factors,
        norm,
        groups,
    )
    return lax.psum_scatter(sums, "ops", scatter_dimension=0, tiled=True)


def solution(mesh):
    placed = (P(("tm", "ops"), None, None),) + (P(),) * 10
    return jax.shard_map(
        body, mesh=mesh, in_specs=placed, out_specs=P(("tm", "ops"), None, None), check_vma=False
    )
```

```python
import math

import jax
import jax.numpy as jnp
from jax import lax
from jax.experimental import pallas as pl
from jax.experimental.pallas import tpu as pltpu
from jax.sharding import PartitionSpec as P


ANY = pl.BlockSpec(memory_space=pl.ANY)
SMEM = pl.BlockSpec(memory_space=pltpu.SMEM)
SIDE = 4
OTHERS = (1, 2, 3)
FAR = ((2, 0), (2, 1))
NEAR = ((1, 0), (1, 1), (3, 0), (3, 1))
HERE = ((0, 1), (0, 0))


def shift_tm(value, dy, dx):
    pairs = [
        (y * SIDE + x, (y + dy) % SIDE * SIDE + (x + dx) % SIDE)
        for y in range(SIDE)
        for x in range(SIDE)
    ]
    return lax.ppermute(value, "tm", pairs)


def shift_ops(value, dz, dc):
    pairs = [
        (z * 2 + core, (z + dz) % SIDE * 2 + (core + dc) % 2)
        for z in range(SIDE)
        for core in range(2)
    ]
    return lax.ppermute(value, "ops", pairs)


def column(table, index):
    return lax.dynamic_slice_in_dim(table.T, index, 1, axis=1)[:, 0]


def look_up(values, keys):
    hits = keys[:, None] == jnp.arange(values.shape[0])[None, :]
    return jnp.sum(jnp.where(hits, values[None, :], 0), axis=1)


def copy_all(copies):
    for copy in copies:
        copy.start()
    for copy in copies:
        copy.wait()


def stack_right(block, stacked, rank):
    stacked[:rank, :] = block
    stacked[rank:, :rank] = -block[:, rank:]
    stacked[rank:, rank:] = block[:, :rank]


def half_shape(nodes, count):
    return jax.ShapeDtypeStruct((count, nodes.shape[1] // 2, nodes.shape[2]), nodes.dtype)


def pick_own(place, wants, nodes, after):
    half = nodes.shape[1] // 2

    def kernel(place_ref, wants_ref, nodes_ref, *refs):
        outs, sems = refs[len(after) : -1], refs[-1]
        y, x = place_ref[0], place_ref[1]
        me = y * SIDE + x
        copies = []
        for n, d in enumerate(OTHERS):
            upper = wants_ref[(y + d) % SIDE * SIDE + x, me]
            lower = wants_ref[y * SIDE + (x + d) % SIDE, me]
            copies.append(
                pltpu.make_async_copy(nodes_ref.at[pl.ds(upper, 1), :half], outs[n], sems.at[n])
            )
            copies.append(
                pltpu.make_async_copy(
                    nodes_ref.at[pl.ds(lower, 1), half:], outs[3 + n], sems.at[3 + n]
                )
            )
        copies.append(
            pltpu.make_async_copy(nodes_ref.at[wants_ref[me, me]], outs[6], sems.at[6])
        )
        copy_all(copies)

    return pl.pallas_call(
        kernel,
        out_shape=[half_shape(nodes, 1)] * 6
        + [jax.ShapeDtypeStruct(nodes.shape[1:], nodes.dtype)],
        in_specs=[SMEM, SMEM, pl.BlockSpec(memory_space=pltpu.VMEM)] + [ANY] * len(after),
        out_specs=[ANY] * 7,
        scratch_shapes=[pltpu.SemaphoreType.DMA((7,))],
        compiler_params=pltpu.CompilerParams(vmem_limit_bytes=6 << 20),
        name="pick_own",
    )(place, wants, nodes, *after)


def pick_relayed(place, wants, across, along):
    def kernel(place_ref, wants_ref, *refs):
        gathered, outs, sems = refs[:12], refs[12:20], refs[20]
        y, x = place_ref[0], place_ref[1]
        waits = []
        for line in range(2):
            for d in range(SIDE):
                for n, behind in enumerate(OTHERS):
                    if line == 0:
                        reader = (y + d) % SIDE * SIDE + x
                        source = y * SIDE + (x + SIDE - behind) % SIDE
                    else:
                        reader = y * SIDE + (x + d) % SIDE
                        source = (y + SIDE - behind) % SIDE * SIDE + x
                    slot = wants_ref[reader, source]
                    low, high = gathered[(line * 3 + n) * 2], gathered[(line * 3 + n) * 2 + 1]
                    target = outs[line * SIDE + d].at[n]
                    sem = sems.at[(line * SIDE + d) * 3 + n]
                    inner = slot % 2

                    @pl.when(slot < 2)
                    def _(low=low, target=target, sem=sem, inner=inner):
                        pltpu.make_async_copy(low.at[inner], target, sem).start()

                    @pl.when(slot >= 2)
                    def _(high=high, target=target, sem=sem, inner=inner):
                        pltpu.make_async_copy(high.at[inner], target, sem).start()

                    waits.append(pltpu.make_async_copy(low.at[0], target, sem))
        for wait in waits:
            wait.wait()

    arrays = [array for pair in across + along for array in pair]
    shape = jax.ShapeDtypeStruct((3,) + arrays[0].shape[1:], arrays[0].dtype)
    outs = pl.pallas_call(
        kernel,
        out_shape=[shape] * 8,
        in_specs=[SMEM, SMEM] + [ANY] * 12,
        out_specs=[ANY] * 8,
        scratch_shapes=[pltpu.SemaphoreType.DMA((24,))],
        compiler_params=pltpu.CompilerParams(vmem_limit_bytes=2 << 20),
        name="pick_relayed",
    )(place, wants, *arrays)
    return outs[:4], outs[4:]


def pair_products(left, right, pieces, outputs, norm):
    own, upper, lower = pieces
    rank, width = own.shape
    half = rank // 2
    upper_line, upper_far, lower_line, lower_far = *upper, *lower

    def kernel(left_ref, right_ref, *refs):
        own_ref, rest = refs[0], refs[1:15]
        outs, (blocks, stacked, sems) = refs[15 : 15 + outputs], refs[15 + outputs :]
        step = pl.program_id(0)

        @pl.when(step == 0)
        def _():
            pairs = [(own_ref, blocks.at[0, 0])]
            for n, d in enumerate(OTHERS):
                pairs.append((rest[n], blocks.at[d, pl.ds(0, 1), :half]))
                pairs.append((rest[7 + n], blocks.at[pl.ds(0, 1), d, half:]))
            for d in range(SIDE):
                pairs.append((rest[3 + d], blocks.at[d, pl.ds(1, 3), :half]))
                pairs.append((rest[10 + d], blocks.at[pl.ds(1, 3), d, half:]))
            copy_all(
                [
                    pltpu.make_async_copy(source, target, sems.at[n])
                    for n, (source, target) in enumerate(pairs)
                ]
            )

        for n, out_ref in enumerate(outs):
            a, b = left_ref[n * 2 + step], right_ref[n * 2 + step]
            stack_right(blocks[b // SIDE, b % SIDE], stacked, rank)
            product = jnp.dot(
                blocks[a // SIDE, a % SIDE], stacked[...], preferred_element_type=jnp.float32
            )
            out_ref[...] = (product * norm).astype(out_ref.dtype)

    return pl.pallas_call(
        kernel,
        out_shape=[jax.ShapeDtypeStruct((2, rank, width), jnp.bfloat16)] * outputs,
        grid_spec=pltpu.PrefetchScalarGridSpec(
            num_scalar_prefetch=2,
            grid=(2,),
            in_specs=[ANY] * 15,
            out_specs=[pl.BlockSpec((None, rank, width), lambda i, l, r: (i, 0, 0))] * outputs,
            scratch_shapes=[
                pltpu.VMEM((SIDE, SIDE, rank, width), jnp.bfloat16),
                pltpu.VMEM((width, width), jnp.bfloat16),
                pltpu.SemaphoreType.DMA((15,)),
            ],
        ),
        compiler_params=pltpu.CompilerParams(vmem_limit_bytes=20 << 20),
        name="pair_products",
    )(left, right, own, *upper_line, *upper_far, *lower_line, *lower_far)


def signed_sums(left, right, target, sign, live, pieces, norm):
    rank, width = pieces[0].shape[1:]
    count = len(pieces)

    def kernel(left_ref, right_ref, target_ref, sign_ref, live_ref, *refs):
        keep_ref, give_ref, blocks, stacked, sums, sems = refs[count:]
        copies = [
            pltpu.make_async_copy(refs[n], blocks.at[pl.ds(2 * n, 2)], sems.at[n])
            for n in range(count)
        ]
        for copy in copies:
            copy.start()
        keep_ref[...] = jnp.zeros_like(keep_ref)
        sums[...] = jnp.zeros_like(sums)
        for copy in copies:
            copy.wait()

        def pair(index, carry):
            stack_right(blocks[right_ref[index]], stacked, rank)
            product = jnp.dot(
                blocks[left_ref[index]], stacked[...], preferred_element_type=jnp.float32
            )
            term = product * (sign_ref[index].astype(jnp.float32) * norm)
            where = target_ref[index]

            @pl.when(where < SIDE)
            def _():
                keep_ref[where % SIDE] += term

            @pl.when(where >= SIDE)
            def _():
                sums[where % SIDE] += term

            return carry

        lax.fori_loop(0, live_ref[0], pair, 0)
        give_ref[...] = sums[...].astype(give_ref.dtype)

    return pl.pallas_call(
        kernel,
        out_shape=[
            jax.ShapeDtypeStruct((SIDE, rank, width), jnp.float32),
            jax.ShapeDtypeStruct((SIDE, rank, width), jnp.bfloat16),
        ],
        in_specs=[SMEM] * 5 + [ANY] * count,
        out_specs=[pl.BlockSpec(memory_space=pltpu.VMEM)] * 2,
        scratch_shapes=[
            pltpu.VMEM((2 * count, rank, width), jnp.bfloat16),
            pltpu.VMEM((width, width), jnp.bfloat16),
            pltpu.VMEM((SIDE, rank, width), jnp.float32),
            pltpu.SemaphoreType.DMA((count,)),
        ],
        compiler_params=pltpu.CompilerParams(vmem_limit_bytes=32 << 20),
        name="signed_sums",
    )(left, right, target, sign, live, *pieces)


def gather_nodes(node_blocks, place, wants):
    half = node_blocks.shape[1] // 2
    upper = [node_blocks[:2, :half], node_blocks[2:, :half]]
    lower = [node_blocks[:2, half:], node_blocks[2:, half:]]
    up, down = {}, {}
    for part in range(2):
        up[1, part] = shift_tm(upper[part], 0, 1)
        down[1, part] = shift_tm(lower[part], 1, 0)
        up[3, 1 - part] = shift_tm(upper[1 - part], 0, 3)
        down[3, 1 - part] = shift_tm(lower[1 - part], 3, 0)
    up[2, 0] = shift_tm(up[1, 0], 0, 1)
    down[2, 0] = shift_tm(down[1, 0], 1, 0)
    up[2, 1] = shift_tm(up[3, 1], 0, 3)
    down[2, 1] = shift_tm(down[3, 1], 3, 0)
    after = [up[1, 1], up[3, 0], down[1, 1], down[3, 0]]
    picked = pick_own(place, wants, node_blocks, after)
    upper_line = [shift_tm(picked[n], d, 0) for n, d in enumerate(OTHERS)]
    lower_line = [shift_tm(picked[3 + n], 0, d) for n, d in enumerate(OTHERS)]
    along_y, along_x = pick_relayed(
        place,
        wants,
        [(up[d, 0], up[d, 1]) for d in OTHERS],
        [(down[d, 0], down[d, 1]) for d in OTHERS],
    )
    far_y, far_x = {0: along_y[0]}, {0: along_x[0]}
    for d in (2, 1, 3):
        far_y[d] = shift_tm(along_y[d], d, 0)
        far_x[d] = shift_tm(along_x[d], 0, d)
    upper_far = [far_y[d] for d in range(SIDE)]
    lower_far = [far_x[d] for d in range(SIDE)]
    return picked[6], (upper_line, upper_far), (lower_line, lower_far)


def body(
    node_blocks,
    first_pulls,
    first_left,
    first_right,
    first_live,
    second_pulls,
    second_left,
    second_right,
    second_live,
    diagram_ids,
    diagram_signs,
):
    times = lax.axis_size("tm")
    groups = lax.axis_size("ops")
    time = lax.axis_index("tm")
    group = lax.axis_index("ops")
    worker = time * groups + group
    y, x = time // SIDE, time % SIDE
    z, core = group // 2, group % 2
    held, rank = node_blocks.shape[:2]
    norm = 1.0 / math.sqrt(2.0 * rank)
    cap = first_left.shape[1]
    reads = second_pulls.shape[1]

    pulls = lax.dynamic_slice_in_dim(
        first_pulls.T.reshape(first_pulls.shape[1], times, groups), group, 1, axis=2
    )[:, :, 0]
    from_time = (pulls // (held * groups))[:, :, None] == jnp.arange(times)[None, None, :]
    wants = jnp.sum(jnp.where(from_time, (pulls % held)[:, :, None], 0), axis=0)
    place = jnp.stack([y, x])
    pieces = gather_nodes(node_blocks, place, wants)

    source = column(first_pulls, worker) // (held * groups)
    source = (y - source // SIDE) % SIDE * SIDE + (x - source % SIDE) % SIDE
    pair_left = look_up(source, column(first_left, worker))
    pair_right = look_up(source, column(first_right, worker))
    row_pulls = lax.dynamic_slice_in_dim(second_pulls.T, time * groups, groups, axis=1)
    coded = jnp.arange(reads)[:, None] * 64 + row_pulls % cap
    mine = row_pulls // cap == worker
    first_pair = jnp.min(jnp.where(mine, coded, reads * 64), axis=0) % 64
    last_pair = jnp.max(jnp.where(mine, coded, 0), axis=0) % 64
    offsets = FAR + NEAR + HERE
    readers = (z + jnp.array([dz for dz, _ in offsets])) % SIDE * 2
    readers = readers + (core + jnp.array([dc for _, dc in offsets])) % 2
    wanted = jnp.stack([look_up(first_pair, readers), look_up(last_pair, readers)], axis=1)
    wanted = wanted.reshape(-1)
    left, right = look_up(pair_left, wanted), look_up(pair_right, wanted)
    arrived = {}
    done = 0
    for part in (FAR, NEAR, HERE):
        here = slice(2 * done, 2 * (done + len(part)))
        products = pair_products(left[here], right[here], pieces, len(part), norm)
        for offset, product in zip(part, products):
            arrived[offset] = product if offset == (0, 0) else shift_ops(product, *offset)
        done += len(part)

    source = column(second_pulls, worker) // cap % groups
    earlier = jnp.arange(reads)[:, None] > jnp.arange(reads)[None, :]
    again = jnp.any(jnp.logical_and(source[:, None] == source[None, :], earlier), axis=1)
    offset = (z - source // 2) % SIDE * 2 + (core + source) % 2
    slot = offset * 2 + again.astype(jnp.int32)
    target = column(diagram_ids, worker) - time * groups
    target = (target // 2 - z) % SIDE + (target + core) % 2 * SIDE
    keep, give = signed_sums(
        look_up(slot, column(second_left, worker)),
        look_up(slot, column(second_right, worker)),
        target,
        column(diagram_signs, worker),
        lax.dynamic_slice_in_dim(second_live, worker, 1),
        [arrived[dz, dc] for dz in range(SIDE) for dc in range(2)],
        norm,
    )
    both = keep + shift_ops(give, 0, 1).astype(jnp.float32)
    total = both[0]
    parts = {d: shift_ops(both[d].astype(jnp.bfloat16), d, 0) for d in (2, 1, 3)}
    for d in OTHERS:
        total = total + parts[d].astype(jnp.float32)
    return total[None]


def solution(mesh):
    placed = (P(("tm", "ops"), None, None),) + (P(),) * 10
    return jax.shard_map(
        body, mesh=mesh, in_specs=placed, out_specs=P(("tm", "ops"), None, None), check_vma=False
    )
```

```python
import math

import jax
import jax.numpy as jnp
from jax import lax
from jax.experimental import pallas as pl
from jax.experimental.pallas import tpu as pltpu
from jax.sharding import PartitionSpec as P


ANY = pl.BlockSpec(memory_space=pl.ANY)
SMEM = pl.BlockSpec(memory_space=pltpu.SMEM)
SIDE = 4
OTHERS = (1, 2, 3)
FAR = ((2, 0), (2, 1))
NEAR = ((1, 0), (1, 1), (3, 0), (3, 1))
HERE = ((0, 1), (0, 0))


def shift_tm(value, dy, dx):
    pairs = [
        (y * SIDE + x, (y + dy) % SIDE * SIDE + (x + dx) % SIDE)
        for y in range(SIDE)
        for x in range(SIDE)
    ]
    return lax.ppermute(value, "tm", pairs)


def shift_ops(value, dz, dc):
    pairs = [
        (z * 2 + core, (z + dz) % SIDE * 2 + (core + dc) % 2)
        for z in range(SIDE)
        for core in range(2)
    ]
    return lax.ppermute(value, "ops", pairs)


def column(table, index):
    return lax.dynamic_slice_in_dim(table.T, index, 1, axis=1)[:, 0]


def look_up(values, keys):
    hits = keys[:, None] == jnp.arange(values.shape[0])[None, :]
    return jnp.sum(jnp.where(hits, values[None, :], 0), axis=1)


def copy_all(copies):
    for copy in copies:
        copy.start()
    for copy in copies:
        copy.wait()


def stack_right(block, stacked, rank):
    stacked[:rank, :] = block
    stacked[rank:, :rank] = -block[:, rank:]
    stacked[rank:, rank:] = block[:, :rank]


def half_shape(nodes, count):
    return jax.ShapeDtypeStruct((count, nodes.shape[1] // 2, nodes.shape[2]), nodes.dtype)


def pick_own(place, wants, nodes):
    half = nodes.shape[1] // 2

    def kernel(place_ref, wants_ref, nodes_ref, *refs):
        outs, sems = refs[:-1], refs[-1]
        y, x = place_ref[0], place_ref[1]
        me = y * SIDE + x
        copies = []
        for n, d in enumerate(OTHERS):
            upper = wants_ref[(y + d) % SIDE * SIDE + x, me]
            lower = wants_ref[y * SIDE + (x + d) % SIDE, me]
            copies.append(
                pltpu.make_async_copy(nodes_ref.at[pl.ds(upper, 1), :half], outs[n], sems.at[n])
            )
            copies.append(
                pltpu.make_async_copy(
                    nodes_ref.at[pl.ds(lower, 1), half:], outs[3 + n], sems.at[3 + n]
                )
            )
        copies.append(
            pltpu.make_async_copy(nodes_ref.at[wants_ref[me, me]], outs[6], sems.at[6])
        )
        copy_all(copies)

    return pl.pallas_call(
        kernel,
        out_shape=[half_shape(nodes, 1)] * 6
        + [jax.ShapeDtypeStruct(nodes.shape[1:], nodes.dtype)],
        in_specs=[SMEM, SMEM, pl.BlockSpec(memory_space=pltpu.VMEM)],
        out_specs=[ANY] * 7,
        scratch_shapes=[pltpu.SemaphoreType.DMA((7,))],
        compiler_params=pltpu.CompilerParams(vmem_limit_bytes=6 << 20),
        name="pick_own",
    )(place, wants, nodes)


def pick_relayed(place, wants, across, along):
    def kernel(place_ref, wants_ref, *refs):
        gathered, outs, sems = refs[:12], refs[12:20], refs[20]
        y, x = place_ref[0], place_ref[1]
        waits = []
        for line in range(2):
            for d in range(SIDE):
                for n, behind in enumerate(OTHERS):
                    if line == 0:
                        reader = (y + d) % SIDE * SIDE + x
                        source = y * SIDE + (x + SIDE - behind) % SIDE
                    else:
                        reader = y * SIDE + (x + d) % SIDE
                        source = (y + SIDE - behind) % SIDE * SIDE + x
                    slot = wants_ref[reader, source]
                    low, high = gathered[(line * 3 + n) * 2], gathered[(line * 3 + n) * 2 + 1]
                    target = outs[line * SIDE + d].at[n]
                    sem = sems.at[(line * SIDE + d) * 3 + n]
                    inner = slot % 2

                    @pl.when(slot < 2)
                    def _(low=low, target=target, sem=sem, inner=inner):
                        pltpu.make_async_copy(low.at[inner], target, sem).start()

                    @pl.when(slot >= 2)
                    def _(high=high, target=target, sem=sem, inner=inner):
                        pltpu.make_async_copy(high.at[inner], target, sem).start()

                    waits.append(pltpu.make_async_copy(low.at[0], target, sem))
        for wait in waits:
            wait.wait()

    arrays = [array for pair in across + along for array in pair]
    shape = jax.ShapeDtypeStruct((3,) + arrays[0].shape[1:], arrays[0].dtype)
    outs = pl.pallas_call(
        kernel,
        out_shape=[shape] * 8,
        in_specs=[SMEM, SMEM] + [pl.BlockSpec(memory_space=pltpu.VMEM)] * 12,
        out_specs=[ANY] * 8,
        scratch_shapes=[pltpu.SemaphoreType.DMA((24,))],
        compiler_params=pltpu.CompilerParams(vmem_limit_bytes=9 << 20),
        name="pick_relayed",
    )(place, wants, *arrays)
    return outs[:4], outs[4:]


def pair_products(left, right, pieces, outputs, norm):
    own, upper, lower = pieces
    rank, width = own.shape
    half = rank // 2
    upper_line, upper_far, lower_line, lower_far = *upper, *lower

    def kernel(left_ref, right_ref, *refs):
        own_ref, rest = refs[0], refs[1:15]
        outs, (blocks, stacked, sems) = refs[15 : 15 + outputs], refs[15 + outputs :]
        step = pl.program_id(0)

        @pl.when(step == 0)
        def _():
            pairs = [(own_ref, blocks.at[0, 0])]
            for n, d in enumerate(OTHERS):
                pairs.append((rest[n], blocks.at[d, pl.ds(0, 1), :half]))
                pairs.append((rest[7 + n], blocks.at[pl.ds(0, 1), d, half:]))
            for d in range(SIDE):
                pairs.append((rest[3 + d], blocks.at[d, pl.ds(1, 3), :half]))
                pairs.append((rest[10 + d], blocks.at[pl.ds(1, 3), d, half:]))
            copy_all(
                [
                    pltpu.make_async_copy(source, target, sems.at[n])
                    for n, (source, target) in enumerate(pairs)
                ]
            )

        for n, out_ref in enumerate(outs):
            a, b = left_ref[n * 2 + step], right_ref[n * 2 + step]
            stack_right(blocks[b // SIDE, b % SIDE], stacked, rank)
            product = jnp.dot(
                blocks[a // SIDE, a % SIDE], stacked[...], preferred_element_type=jnp.float32
            )
            out_ref[...] = (product * norm).astype(out_ref.dtype)

    return pl.pallas_call(
        kernel,
        out_shape=[jax.ShapeDtypeStruct((2, rank, width), jnp.bfloat16)] * outputs,
        grid_spec=pltpu.PrefetchScalarGridSpec(
            num_scalar_prefetch=2,
            grid=(2,),
            in_specs=[ANY] * 15,
            out_specs=[pl.BlockSpec((None, rank, width), lambda i, l, r: (i, 0, 0))] * outputs,
            scratch_shapes=[
                pltpu.VMEM((SIDE, SIDE, rank, width), jnp.bfloat16),
                pltpu.VMEM((width, width), jnp.bfloat16),
                pltpu.SemaphoreType.DMA((15,)),
            ],
        ),
        compiler_params=pltpu.CompilerParams(vmem_limit_bytes=20 << 20),
        name="pair_products",
    )(left, right, own, *upper_line, *upper_far, *lower_line, *lower_far)


def signed_sums(left, right, target, sign, live, pieces, norm):
    rank, width = pieces[0].shape[1:]
    count = len(pieces)

    def kernel(left_ref, right_ref, target_ref, sign_ref, live_ref, *refs):
        keep_ref, give_ref, blocks, stacked, sums, sems = refs[count:]
        copies = [
            pltpu.make_async_copy(refs[n], blocks.at[pl.ds(2 * n, 2)], sems.at[n])
            for n in range(count)
        ]
        for copy in copies:
            copy.start()
        keep_ref[...] = jnp.zeros_like(keep_ref)
        sums[...] = jnp.zeros_like(sums)
        for copy in copies:
            copy.wait()

        def pair(index, carry):
            stack_right(blocks[right_ref[index]], stacked, rank)
            product = jnp.dot(
                blocks[left_ref[index]], stacked[...], preferred_element_type=jnp.float32
            )
            term = product * (sign_ref[index].astype(jnp.float32) * norm)
            where = target_ref[index]

            @pl.when(where < SIDE)
            def _():
                keep_ref[where % SIDE] += term

            @pl.when(where >= SIDE)
            def _():
                sums[where % SIDE] += term

            return carry

        lax.fori_loop(0, live_ref[0], pair, 0)
        give_ref[...] = sums[...].astype(give_ref.dtype)

    return pl.pallas_call(
        kernel,
        out_shape=[
            jax.ShapeDtypeStruct((SIDE, rank, width), jnp.float32),
            jax.ShapeDtypeStruct((SIDE, rank, width), jnp.bfloat16),
        ],
        in_specs=[SMEM] * 5 + [ANY] * count,
        out_specs=[pl.BlockSpec(memory_space=pltpu.VMEM)] * 2,
        scratch_shapes=[
            pltpu.VMEM((2 * count, rank, width), jnp.bfloat16),
            pltpu.VMEM((width, width), jnp.bfloat16),
            pltpu.VMEM((SIDE, rank, width), jnp.float32),
            pltpu.SemaphoreType.DMA((count,)),
        ],
        compiler_params=pltpu.CompilerParams(vmem_limit_bytes=32 << 20),
        name="signed_sums",
    )(left, right, target, sign, live, *pieces)


def gather_nodes(node_blocks, place, wants):
    half = node_blocks.shape[1] // 2
    upper = [node_blocks[:2, :half], node_blocks[2:, :half]]
    lower = [node_blocks[:2, half:], node_blocks[2:, half:]]
    up, down = {}, {}
    for part in range(2):
        up[1, part] = shift_tm(upper[part], 0, 1)
        down[1, part] = shift_tm(lower[part], 1, 0)
        up[3, 1 - part] = shift_tm(upper[1 - part], 0, 3)
        down[3, 1 - part] = shift_tm(lower[1 - part], 3, 0)
    up[2, 0] = shift_tm(up[1, 0], 0, 1)
    down[2, 0] = shift_tm(down[1, 0], 1, 0)
    up[2, 1] = shift_tm(up[3, 1], 0, 3)
    down[2, 1] = shift_tm(down[3, 1], 3, 0)
    picked = pick_own(place, wants, node_blocks)
    upper_line = [shift_tm(picked[n], d, 0) for n, d in enumerate(OTHERS)]
    lower_line = [shift_tm(picked[3 + n], 0, d) for n, d in enumerate(OTHERS)]
    along_y, along_x = pick_relayed(
        place,
        wants,
        [(up[d, 0], up[d, 1]) for d in OTHERS],
        [(down[d, 0], down[d, 1]) for d in OTHERS],
    )
    far_y, far_x = {0: along_y[0]}, {0: along_x[0]}
    for d in (2, 1, 3):
        far_y[d] = shift_tm(along_y[d], d, 0)
        far_x[d] = shift_tm(along_x[d], 0, d)
    upper_far = [far_y[d] for d in range(SIDE)]
    lower_far = [far_x[d] for d in range(SIDE)]
    return picked[6], (upper_line, upper_far), (lower_line, lower_far)


def body(
    node_blocks,
    first_pulls,
    first_left,
    first_right,
    first_live,
    second_pulls,
    second_left,
    second_right,
    second_live,
    diagram_ids,
    diagram_signs,
):
    times = lax.axis_size("tm")
    groups = lax.axis_size("ops")
    time = lax.axis_index("tm")
    group = lax.axis_index("ops")
    worker = time * groups + group
    y, x = time // SIDE, time % SIDE
    z, core = group // 2, group % 2
    held, rank = node_blocks.shape[:2]
    norm = 1.0 / math.sqrt(2.0 * rank)
    cap = first_left.shape[1]
    reads = second_pulls.shape[1]

    pulls = lax.dynamic_slice_in_dim(
        first_pulls.T.reshape(first_pulls.shape[1], times, groups), group, 1, axis=2
    )[:, :, 0]
    from_time = (pulls // (held * groups))[:, :, None] == jnp.arange(times)[None, None, :]
    wants = jnp.sum(jnp.where(from_time, (pulls % held)[:, :, None], 0), axis=0)
    place = jnp.stack([y, x])
    pieces = gather_nodes(node_blocks, place, wants)

    source = column(first_pulls, worker) // (held * groups)
    source = (y - source // SIDE) % SIDE * SIDE + (x - source % SIDE) % SIDE
    pair_left = look_up(source, column(first_left, worker))
    pair_right = look_up(source, column(first_right, worker))
    row_pulls = lax.dynamic_slice_in_dim(second_pulls.T, time * groups, groups, axis=1)
    coded = jnp.arange(reads)[:, None] * 64 + row_pulls % cap
    mine = row_pulls // cap == worker
    first_pair = jnp.min(jnp.where(mine, coded, reads * 64), axis=0) % 64
    last_pair = jnp.max(jnp.where(mine, coded, 0), axis=0) % 64
    offsets = FAR + NEAR + HERE
    readers = (z + jnp.array([dz for dz, _ in offsets])) % SIDE * 2
    readers = readers + (core + jnp.array([dc for _, dc in offsets])) % 2
    wanted = jnp.stack([look_up(first_pair, readers), look_up(last_pair, readers)], axis=1)
    wanted = wanted.reshape(-1)
    left, right = look_up(pair_left, wanted), look_up(pair_right, wanted)
    arrived = {}
    done = 0
    for part in (FAR, NEAR, HERE):
        here = slice(2 * done, 2 * (done + len(part)))
        products = pair_products(left[here], right[here], pieces, len(part), norm)
        for offset, product in zip(part, products):
            arrived[offset] = product if offset == (0, 0) else shift_ops(product, *offset)
        done += len(part)

    source = column(second_pulls, worker) // cap % groups
    earlier = jnp.arange(reads)[:, None] > jnp.arange(reads)[None, :]
    again = jnp.any(jnp.logical_and(source[:, None] == source[None, :], earlier), axis=1)
    offset = (z - source // 2) % SIDE * 2 + (core + source) % 2
    slot = offset * 2 + again.astype(jnp.int32)
    target = column(diagram_ids, worker) - time * groups
    target = (target // 2 - z) % SIDE + (target + core) % 2 * SIDE
    keep, give = signed_sums(
        look_up(slot, column(second_left, worker)),
        look_up(slot, column(second_right, worker)),
        target,
        column(diagram_signs, worker),
        lax.dynamic_slice_in_dim(second_live, worker, 1),
        [arrived[dz, dc] for dz in range(SIDE) for dc in range(2)],
        norm,
    )
    both = keep + shift_ops(give, 0, 1).astype(jnp.float32)
    total = both[0]
    parts = {d: shift_ops(both[d].astype(jnp.bfloat16), d, 0) for d in (2, 1, 3)}
    for d in OTHERS:
        total = total + parts[d].astype(jnp.float32)
    return total[None]


def solution(mesh):
    placed = (P(("tm", "ops"), None, None),) + (P(),) * 10
    return jax.shard_map(body, mesh=mesh, in_specs=placed, out_specs=P(("tm", "ops"), None, None), check_vma=False)
```

```python
import math

import jax
import jax.numpy as jnp
from jax import lax
from jax.experimental import pallas as pl
from jax.experimental.pallas import tpu as pltpu
from jax.sharding import PartitionSpec as P


ANY = pl.BlockSpec(memory_space=pl.ANY)
SMEM = pl.BlockSpec(memory_space=pltpu.SMEM)
SIDE = 4
OTHERS = (1, 2, 3)
FAR = ((2, 0), (2, 1))
NEAR = ((1, 0), (1, 1), (3, 0), (3, 1))
HERE = ((0, 1), (0, 0))

OWN, RELAY, LEFT, RIGHT, LEFT2, RIGHT2, TARGET, SIGN, LIVE = 0, 8, 32, 48, 64, 80, 96, 112, 128
PLAN_SIZE = 256


def shift_tm(value, dy, dx):
    pairs = [
        (y * SIDE + x, (y + dy) % SIDE * SIDE + (x + dx) % SIDE)
        for y in range(SIDE)
        for x in range(SIDE)
    ]
    return lax.ppermute(value, "tm", pairs)


def shift_ops(value, dz, dc):
    pairs = [
        (z * 2 + core, (z + dz) % SIDE * 2 + (core + dc) % 2)
        for z in range(SIDE)
        for core in range(2)
    ]
    return lax.ppermute(value, "ops", pairs)


def copy_all(copies):
    for copy in copies:
        copy.start()
    for copy in copies:
        copy.wait()


def make_plan(cap, first_pulls, first_left, first_right, second_pulls, second_left, second_right, live, ids, signs):
    reads = second_pulls.shape[1]

    def kernel(pulls, left, right, pulls2, left2, right2, live2, ids_ref, signs_ref, plan, slots, pairs, seen, place):
        time, group = lax.axis_index("tm"), lax.axis_index("ops")
        y, x, z, core = time >> 2, time & 3, group >> 1, group & 1
        worker = time * 8 + group

        readers = [(d, 0) for d in range(SIDE)] + [(0, d) for d in OTHERS]
        workers = [
            ((((y + dy) & 3) << 2) + ((x + dx) & 3)) * 8 + group for dy, dx in readers
        ]

        def invert(j, carry):
            for r, reader in enumerate(workers):
                pull = pulls[j, reader]
                slots[r, pull >> 5] = pull & 3
            return carry

        lax.fori_loop(0, pulls.shape[0], invert, 0)
        for n, d in enumerate(OTHERS):
            plan[OWN + n] = slots[d, time]
            plan[OWN + 3 + n] = slots[3 + d, time]
        plan[OWN + 6] = slots[0, time]
        for n, behind in enumerate(OTHERS):
            source_x = (y << 2) + ((x - behind) & 3)
            source_y = (((y - behind) & 3) << 2) + x
            for d in range(SIDE):
                plan[RELAY + d * 3 + n] = slots[d, source_x]
                plan[RELAY + (SIDE + d) * 3 + n] = slots[3 + d if d else 0, source_y]

        for n, (dz, dc) in enumerate(FAR + NEAR + HERE):
            reader = time * 8 + (((z + dz) & 3) << 1) + ((core + dc) & 1)

            def find(j, count, n=n, reader=reader):
                pair = pulls2[j, reader] - worker * cap
                here = jnp.logical_and(pair >= 0, pair < cap)

                @pl.when(here)
                def _():
                    pairs[2 * n + jnp.minimum(count, 1)] = pair

                return count + here.astype(jnp.int32)

            lax.fori_loop(0, reads, find, jnp.int32(0))

        def position(entry):
            source = pulls[entry, worker] >> 5
            return (((y - (source >> 2)) & 3) << 2) + ((x - (source & 3)) & 3)

        def products(n, carry):
            pair = pairs[n]
            plan[LEFT + n] = position(left[pair, worker])
            plan[RIGHT + n] = position(right[pair, worker])
            return carry

        lax.fori_loop(0, 16, products, 0)

        for g in range(8):
            seen[g] = 0

        def arrivals(j, carry):
            source = lax.div(pulls2[j, worker] - time * (8 * cap), jnp.int32(cap))
            offset = (((z - (source >> 1)) & 3) << 1) + ((core + source) & 1)
            earlier = seen[source]
            seen[source] = earlier + 1
            place[j] = offset * 2 + jnp.minimum(earlier, 1)
            return carry

        lax.fori_loop(0, reads, arrivals, 0)

        def terms(q, carry):
            plan[LEFT2 + q] = place[left2[q, worker]]
            plan[RIGHT2 + q] = place[right2[q, worker]]
            target = ids_ref[q, worker] - time * 8
            ahead = ((target >> 1) - z) & 3
            order = jnp.where(ahead == 2, 0, jnp.where(ahead == 1, 1, jnp.where(ahead == 3, 2, 3)))
            plan[TARGET + q] = order + ((target + core) & 1) * SIDE
            plan[SIGN + q] = signs_ref[q, worker]
            return carry

        lax.fori_loop(0, left2.shape[0], terms, 0)
        plan[LIVE] = live2[worker]

    return pl.pallas_call(
        kernel,
        out_shape=jax.ShapeDtypeStruct((PLAN_SIZE,), jnp.int32),
        in_specs=[SMEM] * 9,
        out_specs=SMEM,
        scratch_shapes=[
            pltpu.SMEM((8, 16), jnp.int32),
            pltpu.SMEM((16,), jnp.int32),
            pltpu.SMEM((8,), jnp.int32),
            pltpu.SMEM((16,), jnp.int32),
        ],
        compiler_params=pltpu.CompilerParams(vmem_limit_bytes=1 << 20),
        name="make_plan",
    )(first_pulls.T, first_left.T, first_right.T, second_pulls.T, second_left.T, second_right.T, live, ids.T, signs.T)


def stack_right(block, stacked, rank):
    stacked[:rank, :] = block
    stacked[rank:, :rank] = -block[:, rank:]
    stacked[rank:, rank:] = block[:, :rank]


def half_shape(nodes, count):
    return jax.ShapeDtypeStruct((count, nodes.shape[1] // 2, nodes.shape[2]), nodes.dtype)


def pick_own(plan, nodes):
    half = nodes.shape[1] // 2

    def kernel(plan_ref, nodes_ref, *refs):
        outs, sems = refs[:-1], refs[-1]
        copies = []
        for n in range(3):
            upper, lower = plan_ref[OWN + n], plan_ref[OWN + 3 + n]
            copies.append(
                pltpu.make_async_copy(nodes_ref.at[pl.ds(upper, 1), :half], outs[n], sems.at[n])
            )
            copies.append(
                pltpu.make_async_copy(
                    nodes_ref.at[pl.ds(lower, 1), half:], outs[3 + n], sems.at[3 + n]
                )
            )
        copies.append(
            pltpu.make_async_copy(nodes_ref.at[plan_ref[OWN + 6]], outs[6], sems.at[6])
        )
        copy_all(copies)

    return pl.pallas_call(
        kernel,
        out_shape=[half_shape(nodes, 1)] * 6
        + [jax.ShapeDtypeStruct(nodes.shape[1:], nodes.dtype)],
        in_specs=[SMEM, pl.BlockSpec(memory_space=pltpu.VMEM)],
        out_specs=[ANY] * 7,
        scratch_shapes=[pltpu.SemaphoreType.DMA((7,))],
        compiler_params=pltpu.CompilerParams(vmem_limit_bytes=6 << 20),
        name="pick_own",
    )(plan, nodes)


def pick_relayed(plan, across, along):
    def kernel(plan_ref, *refs):
        gathered, outs, sems = refs[:12], refs[12:20], refs[20]
        waits = []
        for line in range(2):
            for d in range(SIDE):
                for n in range(3):
                    slot = plan_ref[RELAY + (line * SIDE + d) * 3 + n]
                    low, high = gathered[(line * 3 + n) * 2], gathered[(line * 3 + n) * 2 + 1]
                    target = outs[line * SIDE + d].at[n]
                    sem = sems.at[(line * SIDE + d) * 3 + n]
                    inner = slot & 1

                    @pl.when(slot < 2)
                    def _(low=low, target=target, sem=sem, inner=inner):
                        pltpu.make_async_copy(low.at[inner], target, sem).start()

                    @pl.when(slot >= 2)
                    def _(high=high, target=target, sem=sem, inner=inner):
                        pltpu.make_async_copy(high.at[inner], target, sem).start()

                    waits.append(pltpu.make_async_copy(low.at[0], target, sem))
        for wait in waits:
            wait.wait()

    arrays = [array for pair in across + along for array in pair]
    shape = jax.ShapeDtypeStruct((3,) + arrays[0].shape[1:], arrays[0].dtype)
    outs = pl.pallas_call(
        kernel,
        out_shape=[shape] * 8,
        in_specs=[SMEM] + [pl.BlockSpec(memory_space=pltpu.VMEM)] * 12,
        out_specs=[ANY] * 8,
        scratch_shapes=[pltpu.SemaphoreType.DMA((24,))],
        compiler_params=pltpu.CompilerParams(vmem_limit_bytes=9 << 20),
        name="pick_relayed",
    )(plan, *arrays)
    return outs[:4], outs[4:]


def pair_products(plan, first, outputs, pieces, norm):
    own, upper, lower = pieces
    rank, width = own.shape
    half = rank // 2
    upper_line, upper_far, lower_line, lower_far = *upper, *lower

    def kernel(plan_ref, *refs):
        own_ref, rest = refs[0], refs[1:15]
        outs, (blocks, stacked, sems) = refs[15 : 15 + outputs], refs[15 + outputs :]
        step = pl.program_id(0)

        @pl.when(step == 0)
        def _():
            pairs = [(own_ref, blocks.at[0, 0])]
            for n, d in enumerate(OTHERS):
                pairs.append((rest[n], blocks.at[d, pl.ds(0, 1), :half]))
                pairs.append((rest[7 + n], blocks.at[pl.ds(0, 1), d, half:]))
            for d in range(SIDE):
                pairs.append((rest[3 + d], blocks.at[d, pl.ds(1, 3), :half]))
                pairs.append((rest[10 + d], blocks.at[pl.ds(1, 3), d, half:]))
            copy_all(
                [
                    pltpu.make_async_copy(source, target, sems.at[n])
                    for n, (source, target) in enumerate(pairs)
                ]
            )

        for n, out_ref in enumerate(outs):
            index = first + n * 2 + step
            a, b = plan_ref[LEFT + index], plan_ref[RIGHT + index]
            stack_right(blocks[b >> 2, b & 3], stacked, rank)
            product = jnp.dot(
                blocks[a >> 2, a & 3], stacked[...], preferred_element_type=jnp.float32
            )
            out_ref[...] = (product * norm).astype(out_ref.dtype)

    return pl.pallas_call(
        kernel,
        out_shape=[jax.ShapeDtypeStruct((2, rank, width), jnp.bfloat16)] * outputs,
        grid=(2,),
        in_specs=[SMEM] + [ANY] * 15,
        out_specs=[pl.BlockSpec((None, rank, width), lambda i: (i, 0, 0))] * outputs,
        scratch_shapes=[
            pltpu.VMEM((SIDE, SIDE, rank, width), jnp.bfloat16),
            pltpu.VMEM((width, width), jnp.bfloat16),
            pltpu.SemaphoreType.DMA((15,)),
        ],
        compiler_params=pltpu.CompilerParams(vmem_limit_bytes=20 << 20),
        name="pair_products",
    )(plan, own, *upper_line, *upper_far, *lower_line, *lower_far)


def signed_sums(plan, first, targets, pieces, norm):
    rank, width = pieces[0].shape[1:]
    count = len(pieces)

    def kernel(plan_ref, *refs):
        keep_ref, give_ref, blocks, stacked, sums, sems = refs[count:]
        copies = [
            pltpu.make_async_copy(refs[n], blocks.at[pl.ds(2 * n, 2)], sems.at[n])
            for n in range(count)
        ]
        for copy in copies:
            copy.start()
        keep_ref[...] = jnp.zeros_like(keep_ref)
        sums[...] = jnp.zeros_like(sums)
        for copy in copies:
            copy.wait()

        def pair(index, carry):
            code = plan_ref[TARGET + index]
            where = (code & 3) - first

            @pl.when(jnp.logical_and(where >= 0, where < targets))
            def _():
                stack_right(blocks[plan_ref[RIGHT2 + index]], stacked, rank)
                product = jnp.dot(
                    blocks[plan_ref[LEFT2 + index]],
                    stacked[...],
                    preferred_element_type=jnp.float32,
                )
                term = product * (plan_ref[SIGN + index].astype(jnp.float32) * norm)

                @pl.when(code < SIDE)
                def _():
                    keep_ref[where] += term

                @pl.when(code >= SIDE)
                def _():
                    sums[where] += term

            return carry

        lax.fori_loop(0, plan_ref[LIVE], pair, 0)
        give_ref[...] = sums[...].astype(give_ref.dtype)

    return pl.pallas_call(
        kernel,
        out_shape=[
            jax.ShapeDtypeStruct((targets, rank, width), jnp.float32),
            jax.ShapeDtypeStruct((targets, rank, width), jnp.bfloat16),
        ],
        in_specs=[SMEM] + [ANY] * count,
        out_specs=[pl.BlockSpec(memory_space=pltpu.VMEM)] * 2,
        scratch_shapes=[
            pltpu.VMEM((2 * count, rank, width), jnp.bfloat16),
            pltpu.VMEM((width, width), jnp.bfloat16),
            pltpu.VMEM((targets, rank, width), jnp.float32),
            pltpu.SemaphoreType.DMA((count,)),
        ],
        compiler_params=pltpu.CompilerParams(vmem_limit_bytes=28 << 20),
    )(plan, *pieces)


def gather_nodes(node_blocks, plan):
    half = node_blocks.shape[1] // 2
    upper = [node_blocks[:2, :half], node_blocks[2:, :half]]
    lower = [node_blocks[:2, half:], node_blocks[2:, half:]]
    up, down = {}, {}
    for part in range(2):
        up[1, part] = shift_tm(upper[part], 0, 1)
        down[1, part] = shift_tm(lower[part], 1, 0)
        up[3, 1 - part] = shift_tm(upper[1 - part], 0, 3)
        down[3, 1 - part] = shift_tm(lower[1 - part], 3, 0)
    up[2, 0] = shift_tm(up[1, 0], 0, 1)
    down[2, 0] = shift_tm(down[1, 0], 1, 0)
    up[2, 1] = shift_tm(up[3, 1], 0, 3)
    down[2, 1] = shift_tm(down[3, 1], 3, 0)
    picked = pick_own(plan, node_blocks)
    upper_line = [shift_tm(picked[n], d, 0) for n, d in enumerate(OTHERS)]
    lower_line = [shift_tm(picked[3 + n], 0, d) for n, d in enumerate(OTHERS)]
    along_y, along_x = pick_relayed(
        plan,
        [(up[d, 0], up[d, 1]) for d in OTHERS],
        [(down[d, 0], down[d, 1]) for d in OTHERS],
    )
    far_y, far_x = {0: along_y[0]}, {0: along_x[0]}
    for d in (2, 1, 3):
        far_y[d] = shift_tm(along_y[d], d, 0)
        far_x[d] = shift_tm(along_x[d], 0, d)
    upper_far = [far_y[d] for d in range(SIDE)]
    lower_far = [far_x[d] for d in range(SIDE)]
    return picked[6], (upper_line, upper_far), (lower_line, lower_far)


def body(
    node_blocks,
    first_pulls,
    first_left,
    first_right,
    first_live,
    second_pulls,
    second_left,
    second_right,
    second_live,
    diagram_ids,
    diagram_signs,
):
    norm = 1.0 / math.sqrt(2.0 * node_blocks.shape[1])
    plan = make_plan(
        first_left.shape[1],
        first_pulls,
        first_left,
        first_right,
        second_pulls,
        second_left,
        second_right,
        second_live,
        diagram_ids,
        diagram_signs,
    )
    pieces = gather_nodes(node_blocks, plan)
    arrived = {}
    done = 0
    for part in (FAR, NEAR, HERE):
        products = pair_products(plan, 2 * done, len(part), pieces, norm)
        for (dz, dc), product in zip(part, products):
            arrived[dz, dc] = product if (dz, dc) == (0, 0) else shift_ops(product, dz, dc)
        done += len(part)

    factors = [arrived[dz, dc] for dz in range(SIDE) for dc in range(2)]
    keep, give = signed_sums(plan, 0, 1, factors, norm)
    both = keep[0] + shift_ops(give[0], 0, 1).astype(jnp.float32)
    far = shift_ops(both.astype(jnp.bfloat16), 2, 0)
    keep, give = signed_sums(plan, 1, 3, factors, norm)
    both = keep + shift_ops(give, 0, 1).astype(jnp.float32)
    near = both.astype(jnp.bfloat16)
    total = both[2] + far.astype(jnp.float32)
    for n, dz in ((0, 1), (1, 3)):
        total = total + shift_ops(near[n], dz, 0).astype(jnp.float32)
    return total[None]


def solution(mesh):
    placed = (P(("tm", "ops"), None, None),) + (P(),) * 10
    return jax.shard_map(body, mesh=mesh, in_specs=placed, out_specs=P(("tm", "ops"), None, None), check_vma=False)
```

```python
import math

import jax
import jax.numpy as jnp
from jax import lax
from jax.experimental import pallas as pl
from jax.experimental.pallas import tpu as pltpu
from jax.sharding import PartitionSpec as P


ANY = pl.BlockSpec(memory_space=pl.ANY)
SMEM = pl.BlockSpec(memory_space=pltpu.SMEM)
SIDE = 4
OTHERS = (1, 2, 3)
FAR = ((2, 0), (2, 1))
NEAR = ((1, 0), (3, 0), (1, 1), (3, 1))
LAST = ((1, 1), (3, 1))
HERE = ((0, 1), (0, 0))

OWN, RELAY, LEFT, RIGHT, LEFT2, RIGHT2, TARGET, SIGN, LIVE = 0, 8, 32, 48, 64, 80, 96, 112, 128
PLAN_SIZE = 256
LATE = 8


def shift_tm(value, dy, dx):
    pairs = [
        (y * SIDE + x, (y + dy) % SIDE * SIDE + (x + dx) % SIDE)
        for y in range(SIDE)
        for x in range(SIDE)
    ]
    return lax.ppermute(value, "tm", pairs)


def shift_ops(value, dz, dc):
    pairs = [
        (z * 2 + core, (z + dz) % SIDE * 2 + (core + dc) % 2)
        for z in range(SIDE)
        for core in range(2)
    ]
    return lax.ppermute(value, "ops", pairs)


def copy_all(copies):
    for copy in copies:
        copy.start()
    for copy in copies:
        copy.wait()


def make_plan(cap, first_pulls, first_left, first_right, second_pulls, second_left, second_right, live, ids, signs):
    reads = second_pulls.shape[1]

    def kernel(pulls, left, right, pulls2, left2, right2, live2, ids_ref, signs_ref, plan, slots, pairs, seen, place):
        time, group = lax.axis_index("tm"), lax.axis_index("ops")
        y, x, z, core = time >> 2, time & 3, group >> 1, group & 1
        worker = time * 8 + group

        readers = [(d, 0) for d in range(SIDE)] + [(0, d) for d in OTHERS]
        workers = [
            ((((y + dy) & 3) << 2) + ((x + dx) & 3)) * 8 + group for dy, dx in readers
        ]

        def invert(j, carry):
            for r, reader in enumerate(workers):
                pull = pulls[j, reader]
                slots[r, pull >> 5] = pull & 3
            return carry

        lax.fori_loop(0, pulls.shape[0], invert, 0)
        for n, d in enumerate(OTHERS):
            plan[OWN + n] = slots[d, time]
            plan[OWN + 3 + n] = slots[3 + d, time]
        plan[OWN + 6] = slots[0, time]
        for n, behind in enumerate(OTHERS):
            source_x = (y << 2) + ((x - behind) & 3)
            source_y = (((y - behind) & 3) << 2) + x
            for d in range(SIDE):
                plan[RELAY + d * 3 + n] = slots[d, source_x]
                plan[RELAY + (SIDE + d) * 3 + n] = slots[3 + d if d else 0, source_y]

        for n, (dz, dc) in enumerate(FAR + NEAR + HERE):
            reader = time * 8 + (((z + dz) & 3) << 1) + ((core + dc) & 1)

            def find(j, count, n=n, reader=reader):
                pair = pulls2[j, reader] - worker * cap
                here = jnp.logical_and(pair >= 0, pair < cap)

                @pl.when(here)
                def _():
                    pairs[2 * n + jnp.minimum(count, 1)] = pair

                return count + here.astype(jnp.int32)

            lax.fori_loop(0, reads, find, jnp.int32(0))

        def position(entry):
            source = pulls[entry, worker] >> 5
            return (((y - (source >> 2)) & 3) << 2) + ((x - (source & 3)) & 3)

        def products(n, carry):
            pair = pairs[n]
            plan[LEFT + n] = position(left[pair, worker])
            plan[RIGHT + n] = position(right[pair, worker])
            return carry

        lax.fori_loop(0, 16, products, 0)

        for g in range(8):
            seen[g] = 0

        def arrivals(j, carry):
            source = lax.div(pulls2[j, worker] - time * (8 * cap), jnp.int32(cap))
            offset = (((z - (source >> 1)) & 3) << 1) + ((core + source) & 1)
            earlier = seen[source]
            seen[source] = earlier + 1
            place[j] = offset * 2 + jnp.minimum(earlier, 1)
            return carry

        lax.fori_loop(0, reads, arrivals, 0)

        def terms(q, carry):
            a, b = place[left2[q, worker]], place[right2[q, worker]]
            plan[LEFT2 + q] = a
            plan[RIGHT2 + q] = b
            late = jnp.logical_or((a >> 1) & 3 == 3, (b >> 1) & 3 == 3).astype(jnp.int32)
            target = ids_ref[q, worker] - time * 8
            ahead = ((target >> 1) - z) & 3
            order = jnp.where(ahead == 2, 0, jnp.where(ahead == 1, 1, jnp.where(ahead == 3, 2, 3)))
            plan[TARGET + q] = order + ((target + core) & 1) * SIDE + late * LATE
            plan[SIGN + q] = signs_ref[q, worker]
            return carry

        lax.fori_loop(0, left2.shape[0], terms, 0)
        plan[LIVE] = live2[worker]

    return pl.pallas_call(
        kernel,
        out_shape=jax.ShapeDtypeStruct((PLAN_SIZE,), jnp.int32),
        in_specs=[SMEM] * 9,
        out_specs=SMEM,
        scratch_shapes=[
            pltpu.SMEM((8, 16), jnp.int32),
            pltpu.SMEM((16,), jnp.int32),
            pltpu.SMEM((8,), jnp.int32),
            pltpu.SMEM((16,), jnp.int32),
        ],
        compiler_params=pltpu.CompilerParams(vmem_limit_bytes=1 << 20),
        name="make_plan",
    )(first_pulls.T, first_left.T, first_right.T, second_pulls.T, second_left.T, second_right.T, live, ids.T, signs.T)


def stack_right(block, stacked, rank):
    stacked[:rank, :] = block
    stacked[rank:, :rank] = -block[:, rank:]
    stacked[rank:, rank:] = block[:, :rank]


def half_shape(nodes, count):
    return jax.ShapeDtypeStruct((count, nodes.shape[1] // 2, nodes.shape[2]), nodes.dtype)


def pick_own(plan, nodes):
    half = nodes.shape[1] // 2

    def kernel(plan_ref, nodes_ref, *refs):
        outs, sems = refs[:-1], refs[-1]
        copies = []
        for n in range(3):
            upper, lower = plan_ref[OWN + n], plan_ref[OWN + 3 + n]
            copies.append(
                pltpu.make_async_copy(nodes_ref.at[pl.ds(upper, 1), :half], outs[n], sems.at[n])
            )
            copies.append(
                pltpu.make_async_copy(
                    nodes_ref.at[pl.ds(lower, 1), half:], outs[3 + n], sems.at[3 + n]
                )
            )
        copies.append(
            pltpu.make_async_copy(nodes_ref.at[plan_ref[OWN + 6]], outs[6], sems.at[6])
        )
        copy_all(copies)

    return pl.pallas_call(
        kernel,
        out_shape=[half_shape(nodes, 1)] * 6
        + [jax.ShapeDtypeStruct(nodes.shape[1:], nodes.dtype)],
        in_specs=[SMEM, pl.BlockSpec(memory_space=pltpu.VMEM)],
        out_specs=[ANY] * 7,
        scratch_shapes=[pltpu.SemaphoreType.DMA((7,))],
        compiler_params=pltpu.CompilerParams(vmem_limit_bytes=6 << 20),
        name="pick_own",
    )(plan, nodes)


def pick_relayed(plan, across, along):
    def kernel(plan_ref, *refs):
        gathered, outs, sems = refs[:12], refs[12:20], refs[20]
        waits = []
        for line in range(2):
            for d in range(SIDE):
                for n in range(3):
                    slot = plan_ref[RELAY + (line * SIDE + d) * 3 + n]
                    low, high = gathered[(line * 3 + n) * 2], gathered[(line * 3 + n) * 2 + 1]
                    target = outs[line * SIDE + d].at[n]
                    sem = sems.at[(line * SIDE + d) * 3 + n]
                    inner = slot & 1

                    @pl.when(slot < 2)
                    def _(low=low, target=target, sem=sem, inner=inner):
                        pltpu.make_async_copy(low.at[inner], target, sem).start()

                    @pl.when(slot >= 2)
                    def _(high=high, target=target, sem=sem, inner=inner):
                        pltpu.make_async_copy(high.at[inner], target, sem).start()

                    waits.append(pltpu.make_async_copy(low.at[0], target, sem))
        for wait in waits:
            wait.wait()

    arrays = [array for pair in across + along for array in pair]
    shape = jax.ShapeDtypeStruct((3,) + arrays[0].shape[1:], arrays[0].dtype)
    outs = pl.pallas_call(
        kernel,
        out_shape=[shape] * 8,
        in_specs=[SMEM] + [pl.BlockSpec(memory_space=pltpu.VMEM)] * 12,
        out_specs=[ANY] * 8,
        scratch_shapes=[pltpu.SemaphoreType.DMA((24,))],
        compiler_params=pltpu.CompilerParams(vmem_limit_bytes=9 << 20),
        name="pick_relayed",
    )(plan, *arrays)
    return outs[:4], outs[4:]


def pair_products(plan, first, outputs, pieces, norm):
    own, upper, lower = pieces
    rank, width = own.shape
    half = rank // 2
    upper_line, upper_far, lower_line, lower_far = *upper, *lower

    def kernel(plan_ref, *refs):
        own_ref, rest = refs[0], refs[1:15]
        outs, (blocks, stacked, sems) = refs[15 : 15 + outputs], refs[15 + outputs :]
        step = pl.program_id(0)

        @pl.when(step == 0)
        def _():
            pairs = [(own_ref, blocks.at[0, 0])]
            for n, d in enumerate(OTHERS):
                pairs.append((rest[n], blocks.at[d, pl.ds(0, 1), :half]))
                pairs.append((rest[7 + n], blocks.at[pl.ds(0, 1), d, half:]))
            for d in range(SIDE):
                pairs.append((rest[3 + d], blocks.at[d, pl.ds(1, 3), :half]))
                pairs.append((rest[10 + d], blocks.at[pl.ds(1, 3), d, half:]))
            copy_all(
                [
                    pltpu.make_async_copy(source, target, sems.at[n])
                    for n, (source, target) in enumerate(pairs)
                ]
            )

        for n, out_ref in enumerate(outs):
            index = first + n * 2 + step
            a, b = plan_ref[LEFT + index], plan_ref[RIGHT + index]
            stack_right(blocks[b >> 2, b & 3], stacked, rank)
            product = jnp.dot(
                blocks[a >> 2, a & 3], stacked[...], preferred_element_type=jnp.float32
            )
            out_ref[...] = (product * norm).astype(out_ref.dtype)

    return pl.pallas_call(
        kernel,
        out_shape=[jax.ShapeDtypeStruct((2, rank, width), jnp.bfloat16)] * outputs,
        grid=(2,),
        in_specs=[SMEM] + [ANY] * 15,
        out_specs=[pl.BlockSpec((None, rank, width), lambda i: (i, 0, 0))] * outputs,
        scratch_shapes=[
            pltpu.VMEM((SIDE, SIDE, rank, width), jnp.bfloat16),
            pltpu.VMEM((width, width), jnp.bfloat16),
            pltpu.SemaphoreType.DMA((15,)),
        ],
        compiler_params=pltpu.CompilerParams(vmem_limit_bytes=20 << 20),
        name="pair_products",
    )(plan, own, *upper_line, *upper_far, *lower_line, *lower_far)


def signed_sums(plan, late, first, targets, pieces, before, norm):
    count = len(pieces)
    here = [n for n in range(count) if pieces[n] is not None]
    given = [pieces[n] for n in here] + list(before)
    rank, width = given[0].shape[1:]

    def kernel(plan_ref, *refs):
        keep_ref, give_ref, blocks, stacked, sums, sems = refs[len(given) :]
        total_ref = sums if before else give_ref
        pairs = [(refs[n], blocks.at[pl.ds(2 * at, 2)]) for n, at in enumerate(here)]
        if before:
            pairs.append((refs[len(here)].at[pl.ds(first, targets)], keep_ref))
            pairs.append((refs[len(here) + 1].at[pl.ds(first, targets)], sums))
        copies = [
            pltpu.make_async_copy(source, target, sems.at[n])
            for n, (source, target) in enumerate(pairs)
        ]
        for copy in copies:
            copy.start()
        if not before:
            keep_ref[...] = jnp.zeros_like(keep_ref)
            give_ref[...] = jnp.zeros_like(give_ref)
        for copy in copies:
            copy.wait()

        def pair(index, carry):
            code = plan_ref[TARGET + index] - late * LATE
            where = (code & 3) - first
            wanted = jnp.logical_and(where >= 0, where < targets)

            @pl.when(jnp.logical_and(wanted, jnp.logical_and(code >= 0, code < LATE)))
            def _():
                stack_right(blocks[plan_ref[RIGHT2 + index]], stacked, rank)
                product = jnp.dot(
                    blocks[plan_ref[LEFT2 + index]],
                    stacked[...],
                    preferred_element_type=jnp.float32,
                )
                term = product * (plan_ref[SIGN + index].astype(jnp.float32) * norm)

                @pl.when(code < SIDE)
                def _():
                    keep_ref[where] += term

                @pl.when(code >= SIDE)
                def _():
                    total_ref[where] += term

            return carry

        lax.fori_loop(0, plan_ref[LIVE], pair, 0)
        if before:
            give_ref[...] = sums[...].astype(give_ref.dtype)

    return pl.pallas_call(
        kernel,
        out_shape=[
            jax.ShapeDtypeStruct((targets, rank, width), jnp.float32),
            jax.ShapeDtypeStruct(
                (targets, rank, width), jnp.bfloat16 if before else jnp.float32
            ),
        ],
        in_specs=[SMEM] + [ANY] * len(given),
        out_specs=[pl.BlockSpec(memory_space=pltpu.VMEM)] * 2,
        scratch_shapes=[
            pltpu.VMEM((2 * count, rank, width), jnp.bfloat16),
            pltpu.VMEM((width, width), jnp.bfloat16),
            pltpu.VMEM((targets if before else 1, rank, width), jnp.float32),
            pltpu.SemaphoreType.DMA((len(given),)),
        ],
        compiler_params=pltpu.CompilerParams(
            vmem_limit_bytes=(22 << 20) if before else (28 << 20)
        ),
    )(plan, *given)


def gather_nodes(node_blocks, plan):
    half = node_blocks.shape[1] // 2
    upper = [node_blocks[:2, :half], node_blocks[2:, :half]]
    lower = [node_blocks[:2, half:], node_blocks[2:, half:]]
    up, down = {}, {}
    for part in range(2):
        up[1, part] = shift_tm(upper[part], 0, 1)
        down[1, part] = shift_tm(lower[part], 1, 0)
        up[3, 1 - part] = shift_tm(upper[1 - part], 0, 3)
        down[3, 1 - part] = shift_tm(lower[1 - part], 3, 0)
    up[2, 0] = shift_tm(up[1, 0], 0, 1)
    down[2, 0] = shift_tm(down[1, 0], 1, 0)
    up[2, 1] = shift_tm(up[3, 1], 0, 3)
    down[2, 1] = shift_tm(down[3, 1], 3, 0)
    picked = pick_own(plan, node_blocks)
    upper_line = [shift_tm(picked[n], d, 0) for n, d in enumerate(OTHERS)]
    lower_line = [shift_tm(picked[3 + n], 0, d) for n, d in enumerate(OTHERS)]
    along_y, along_x = pick_relayed(
        plan,
        [(up[d, 0], up[d, 1]) for d in OTHERS],
        [(down[d, 0], down[d, 1]) for d in OTHERS],
    )
    far_y, far_x = {0: along_y[0]}, {0: along_x[0]}
    for d in (2, 1, 3):
        far_y[d] = shift_tm(along_y[d], d, 0)
        far_x[d] = shift_tm(along_x[d], 0, d)
    upper_far = [far_y[d] for d in range(SIDE)]
    lower_far = [far_x[d] for d in range(SIDE)]
    return picked[6], (upper_line, upper_far), (lower_line, lower_far)


def body(
    node_blocks,
    first_pulls,
    first_left,
    first_right,
    first_live,
    second_pulls,
    second_left,
    second_right,
    second_live,
    diagram_ids,
    diagram_signs,
):
    norm = 1.0 / math.sqrt(2.0 * node_blocks.shape[1])
    plan = make_plan(
        first_left.shape[1],
        first_pulls,
        first_left,
        first_right,
        second_pulls,
        second_left,
        second_right,
        second_live,
        diagram_ids,
        diagram_signs,
    )
    pieces = gather_nodes(node_blocks, plan)
    arrived = {}
    done = 0
    for part in (FAR, NEAR, HERE):
        products = pair_products(plan, 2 * done, len(part), pieces, norm)
        for (dz, dc), product in zip(part, products):
            arrived[dz, dc] = product if (dz, dc) == (0, 0) else shift_ops(product, dz, dc)
        done += len(part)

    offsets = [(dz, dc) for dz in range(SIDE) for dc in range(2)]
    factors = [arrived[offset] for offset in offsets]
    ready = [None if offset in LAST else arrived[offset] for offset in offsets]
    early = signed_sums(plan, 0, 0, SIDE, ready, (), norm)

    def both_cores(first, targets):
        keep, give = signed_sums(plan, 1, first, targets, factors, early, norm)
        return keep + shift_ops(give, 0, 1).astype(jnp.float32)

    far = both_cores(0, 1).astype(jnp.bfloat16)
    parts = [shift_ops(far[0], 2, 0)]
    near = both_cores(1, 2).astype(jnp.bfloat16)
    parts += [shift_ops(near[0], 1, 0), shift_ops(near[1], 3, 0)]
    total = both_cores(3, 1)
    for part in parts:
        total = total + part.astype(jnp.float32)[None]
    return total


def solution(mesh):
    placed = (P(("tm", "ops"), None, None),) + (P(),) * 10
    return jax.shard_map(body, mesh=mesh, in_specs=placed, out_specs=P(("tm", "ops"), None, None), check_vma=False)
```
